128 devices in a mesh: seq: 8 (over x, core), head: 16 (over y, z).
Axes of the slice: x: 4, y: 4, z: 4, core: 2. Of those that a mesh axis runs over, the one named last changes fastest.
Arguments:
- tokens: bfloat16 [2048, 4096], P('seq', 'head'), may hold values from -6 to 6
- w_query: bfloat16 [4096, 2048], P(None, 'head'), may hold values from -0.09375 to 0.09375
- w_key: bfloat16 [4096, 2048], P(None, 'head'), may hold values from -0.09375 to 0.09375
- w_value: bfloat16 [4096, 2048], P(None, 'head'), may hold values from -0.09375 to 0.09375
- w_out: bfloat16 [2048, 4096], P('head'), may hold values from -0.125 to 0.125
- grad_out: bfloat16 [2048, 4096], P('seq', 'head'), may hold values from -6 to 6
- state_in: float32 [16, 128, 128], P('head'), may hold values from -384 to 384
Outputs:
- result: bfloat16 [2048, 4096], P('seq', 'head')
- grad_tokens: float32 [2048, 4096], P('seq', 'head')
- grad_wq: float32 [4096, 2048], P('seq', 'head')
- grad_wk: float32 [4096, 2048], P('seq', 'head')
- grad_wv: float32 [4096, 2048], P('seq', 'head')
- grad_wo: float32 [2048, 4096], P('head', 'seq')
- grad_state_in: float32 [16, 128, 128], P('head')
The draws below stay inside these ranges and needn't reach their ends.
All inputs are finite; a program needn't handle non-finite values.
Results may differ from the reference program's by a relative error of at most 0.018.
Values may be sent and summed in bfloat16 or wider, within the bound.
No kernel may reach another device: no remote copies, remote signals or barrier semaphores. Data moves between devices by JAX's collectives and lax.ppermute only.
A program may use at most 64 MiB of HBM per device.

```python
import jax
import jax.numpy as jnp
from jax import lax

D = 4096
HEADS = 16
DH = 128
BLOCK = 256
TOKENS = 2048
N_HEAD = 16


def block_levels(stream_key, extent, shards, smallest, largest):
    gain, own = 1.0, jax.random.fold_in(stream_key, 6)
    for dim, parts in shards:
        steps = jnp.exp(jax.random.uniform(jax.random.fold_in(own, dim), (parts,), jnp.float32, smallest / len(shards), largest / len(shards)))
        gain = gain * jnp.repeat(steps, extent[dim] // parts).reshape([-1 if axis == dim else 1 for axis in range(len(extent))])
    return gain


def centred(rng, shape, scale, most, cuts=(), kind=jnp.bfloat16):
    drawn = scale * jax.random.normal(rng, shape, jnp.float32)
    if cuts:
        drawn = drawn * block_levels(rng, shape, cuts, -0.22, 0.18)
    return jnp.clip(drawn, -most, most).astype(kind)


def setup_inputs(seed: int = 0) -> dict:
    arg_keys = jax.random.split(jax.random.key(seed), 8)
    return {
        "tokens": centred(arg_keys[0], (TOKENS, D), 1.0, 6.0, ((0, 8), (1, 16))),
        "w_query": centred(arg_keys[1], (D, HEADS * DH), D ** -0.5, 0.09375, ((1, 16),)),
        "w_key": centred(arg_keys[2], (D, HEADS * DH), D ** -0.5, 0.09375, ((1, 16),)),
        "w_value": centred(arg_keys[3], (D, HEADS * DH), D ** -0.5, 0.09375, ((1, 16),)),
        "w_out": centred(arg_keys[4], (HEADS * DH, D), (HEADS * DH) ** -0.5, 0.125, ((0, 16),)),
        "grad_out": centred(arg_keys[5], (TOKENS, D), 1.0, 6.0, ((0, 8), (1, 16))),
        "state_in": centred(arg_keys[6], (HEADS, DH, DH), (DH // 2), 384.0, ((0, 16),), jnp.float32),
    }


EPSILON = 1e-06
WIDE_TYPE = jnp.float32
HALF_TYPE = jnp.bfloat16

def causal_mask(width):
    return jnp.tril(jnp.ones((width, width), WIDE_TYPE)) > 0.5

def excl_prefix(states):
    running = jnp.cumsum(states, axis=0)
    return jnp.concatenate([jnp.zeros_like(states[:1]), running[:-1]], axis=0)

def excl_suffix(states):
    return jnp.flip(excl_prefix(jnp.flip(states, 0)), 0)

def block_scores(query_blk, keys_blk):
    allowed = causal_mask(query_blk.shape[0])
    scores = jnp.einsum('thd,shd->hts', query_blk.astype(WIDE_TYPE), keys_blk.astype(WIDE_TYPE))
    return jnp.where(allowed[None], scores, 0.0).astype(HALF_TYPE)

def forward_block(pieces):
    query_blk, keys_blk, value_blk, prior_bf = pieces
    scores_bf = block_scores(query_blk, keys_blk)
    local_part = jnp.einsum('hts,shd->thd', scores_bf.astype(WIDE_TYPE), value_blk.astype(WIDE_TYPE))
    carried = jnp.einsum('thd,hde->the', query_blk.astype(WIDE_TYPE), prior_bf.astype(WIDE_TYPE))
    return local_part + carried

def backward_block(pieces):
    query_blk, keys_blk, value_blk, grad_mixed, prior_bf, later_bf = pieces
    allowed = causal_mask(query_blk.shape[0])
    scores_bf = block_scores(query_blk, keys_blk).astype(WIDE_TYPE)
    query_w = query_blk.astype(WIDE_TYPE)
    keys_w = keys_blk.astype(WIDE_TYPE)
    value_w = value_blk.astype(WIDE_TYPE)
    grad_w = grad_mixed.astype(WIDE_TYPE)
    prior_w = prior_bf.astype(WIDE_TYPE)
    later_w = later_bf.astype(WIDE_TYPE)
    grad_scores = jnp.einsum('thd,shd->hts', grad_w, value_w)
    grad_scores = jnp.where(allowed[None], grad_scores, 0.0).astype(HALF_TYPE).astype(WIDE_TYPE)
    grad_query = jnp.einsum('hts,shd->thd', grad_scores, keys_w) + jnp.einsum('the,hde->thd', grad_w, prior_w)
    grad_keys = jnp.einsum('hts,thd->shd', grad_scores, query_w) + jnp.einsum('she,hde->shd', value_w, later_w)
    grad_value = jnp.einsum('hts,the->she', scores_bf, grad_w) + jnp.einsum('shd,hde->she', keys_w, later_w)
    return (grad_query.astype(HALF_TYPE), grad_keys.astype(HALF_TYPE), grad_value.astype(HALF_TYPE))

def reference(tokens, w_query, w_key, w_value, w_out, grad_out, state_in):
    group_cols = HEADS * DH // N_HEAD
    blocks = TOKENS // BLOCK
    block_shape = (blocks, BLOCK, HEADS, DH)
    query = jnp.dot(tokens, w_query, preferred_element_type=WIDE_TYPE).astype(HALF_TYPE).reshape(block_shape)
    keys = jnp.dot(tokens, w_key, preferred_element_type=WIDE_TYPE).astype(HALF_TYPE).reshape(block_shape)
    values = jnp.dot(tokens, w_value, preferred_element_type=WIDE_TYPE).astype(HALF_TYPE).reshape(block_shape)
    states = jnp.einsum('cshd,cshe->chde', keys.astype(WIDE_TYPE), values.astype(WIDE_TYPE))
    prior_bf = (state_in[None] + excl_prefix(states)).astype(HALF_TYPE)
    mixed = lax.map(forward_block, (query, keys, values, prior_bf))
    inv_norm = lax.rsqrt(lax.optimization_barrier(jnp.mean(mixed * mixed, axis=-1, keepdims=True)) + EPSILON)
    normed = (mixed * inv_norm).astype(HALF_TYPE).reshape(TOKENS, HEADS * DH)
    out_groups = normed.reshape(TOKENS, N_HEAD, group_cols).transpose(1, 0, 2)
    out_weights = w_out.reshape(N_HEAD, group_cols, D)

    def add_out(running, group_pair):
        piece_out = jnp.dot(group_pair[0], group_pair[1], preferred_element_type=WIDE_TYPE).astype(HALF_TYPE)
        piece_out = lax.optimization_barrier(piece_out)
        return (running + piece_out.astype(WIDE_TYPE), None)
    out_sum, _ = lax.scan(add_out, jnp.zeros((TOKENS, D), WIDE_TYPE), (out_groups, out_weights))
    result = out_sum.astype(HALF_TYPE)
    contract_last = (((1,), (1,)), ((), ()))
    grad_normed = lax.dot_general(grad_out, w_out, contract_last, preferred_element_type=WIDE_TYPE).reshape(block_shape)
    grad_mixed = inv_norm * (grad_normed - mixed * inv_norm * inv_norm * lax.optimization_barrier(jnp.mean(grad_normed * mixed, axis=-1, keepdims=True)))
    grad_mixed = grad_mixed.astype(HALF_TYPE)
    back_states = jnp.einsum('cthd,cthe->chde', query.astype(WIDE_TYPE), grad_mixed.astype(WIDE_TYPE))
    later_bf = excl_suffix(back_states).astype(HALF_TYPE)
    grad_state_in = lax.optimization_barrier(jnp.sum(back_states, axis=0))
    grad_query, grad_keys, grad_value = lax.map(backward_block, (query, keys, values, grad_mixed, prior_bf, later_bf))
    grad_query = grad_query.reshape(TOKENS, HEADS * DH)
    grad_keys = grad_keys.reshape(TOKENS, HEADS * DH)
    grad_value = grad_value.reshape(TOKENS, HEADS * DH)

    def split_cols(matrix):
        return matrix.reshape(matrix.shape[0], N_HEAD, group_cols).transpose(1, 0, 2)

    def add_input(running, group_set):
        piece_in = lax.dot_general(group_set[0], group_set[3], contract_last, preferred_element_type=WIDE_TYPE)
        piece_in = piece_in + lax.dot_general(group_set[1], group_set[4], contract_last, preferred_element_type=WIDE_TYPE)
        piece_in = piece_in + lax.dot_general(group_set[2], group_set[5], contract_last, preferred_element_type=WIDE_TYPE)
        piece_in = lax.optimization_barrier(piece_in.astype(HALF_TYPE))
        return (running + piece_in.astype(WIDE_TYPE), None)
    grad_tokens, _ = lax.scan(add_input, jnp.zeros((TOKENS, D), WIDE_TYPE), (split_cols(grad_query), split_cols(grad_keys), split_cols(grad_value), split_cols(w_query), split_cols(w_key), split_cols(w_value)))
    grad_wq = jnp.dot(tokens.T, grad_query, preferred_element_type=WIDE_TYPE)
    grad_wk = jnp.dot(tokens.T, grad_keys, preferred_element_type=WIDE_TYPE)
    grad_wv = jnp.dot(tokens.T, grad_value, preferred_element_type=WIDE_TYPE)
    grad_wo = jnp.dot(normed.T, grad_out, preferred_element_type=WIDE_TYPE)
    return (result, grad_tokens, grad_wq, grad_wk, grad_wv, grad_wo, grad_state_in)
```

```python
import jax
import jax.numpy as jnp
from jax import lax
from jax.experimental import pallas as pl
from jax.experimental.pallas import tpu as pltpu
from jax.sharding import Mesh
from jax.sharding import PartitionSpec as P

SEQ = ("x", "core")
HEAD = ("y", "z")
PLANE = ("core", "y", "z")
SIDE = 4
EPSILON = 1e-06
WIDE = jnp.float32
HALF = jnp.bfloat16

NN = (((1,), (0,)), ((), ()))
NT = (((1,), (1,)), ((), ()))
TN = (((0,), (0,)), ((), ()))


def mm(a, b, dims):
    return lax.dot_general(a, b, dims, preferred_element_type=WIDE)


def plane_pairs(phase, shift):
    pairs = []
    for core in range(2):
        for y in range(SIDE):
            for z in range(SIDE):
                along_y = core == phase
                ty = (y + shift) % SIDE if along_y else y
                tz = z if along_y else (z + shift) % SIDE
                pairs.append(((core * SIDE + y) * SIDE + z, (core * SIDE + ty) * SIDE + tz))
    return pairs


def plane_shift(a, phase, shift):
    return lax.ppermute(a, PLANE, plane_pairs(phase, shift))


def x_shift(a, shift):
    return lax.ppermute(a, "x", [(i, (i + shift) % SIDE) for i in range(SIDE)])


def core_swap(a):
    return lax.ppermute(a, "core", [(0, 1), (1, 0)])


def block_table():
    core, y, z = (lax.axis_index(n) for n in PLANE)
    at = jnp.arange(SIDE * SIDE, dtype=jnp.int32)
    d2, d1 = at // SIDE, at % SIDE
    dy = jnp.where(core == 0, d1, d2)
    dz = jnp.where(core == 0, d2, d1)
    return ((y - dy) % SIDE) * SIDE + (z - dz) % SIDE


def order_weights_kernel(table, q, k, v, o, qkv_out, o_out):
    n = q.shape[1]
    qkv_out[:, :n] = q[...]
    qkv_out[:, n : 2 * n] = k[...]
    qkv_out[:, 2 * n :] = v[...]
    o_out[...] = o[...].T


def order_weights(table, w_query, w_key, w_value, w_out):
    rows, n = w_query.shape
    blocks = SIDE * SIDE
    step = rows // blocks
    tall = pl.BlockSpec((step, n), lambda i, t: (t[i], 0))
    return pl.pallas_call(
        order_weights_kernel,
        out_shape=(
            jax.ShapeDtypeStruct((rows, 3 * n), HALF),
            jax.ShapeDtypeStruct((rows, n), HALF),
        ),
        grid_spec=pltpu.PrefetchScalarGridSpec(
            num_scalar_prefetch=1,
            grid=(blocks,),
            in_specs=[tall, tall, tall, pl.BlockSpec((n, step), lambda i, t: (0, t[i]))],
            out_specs=[
                pl.BlockSpec((step, 3 * n), lambda i, t: (i, 0)),
                pl.BlockSpec((step, n), lambda i, t: (i, 0)),
            ],
        ),
        cost_estimate=pl.CostEstimate(
            flops=0, bytes_accessed=16 * rows * n, transcendentals=0
        ),
        name="order_weights",
    )(table, w_query, w_key, w_value, w_out)


def place_blocks_kernel(table, a0, a1, a2, a3, out, sem):
    step = a0.shape[0] // SIDE
    copies = []
    for d2, ref in enumerate((a0, a1, a2, a3)):
        for d1 in range(SIDE):
            to = pl.multiple_of(table[d2 * SIDE + d1] * step, step)
            copies.append(
                pltpu.make_async_copy(
                    ref.at[pl.ds(d1 * step, step)], out.at[pl.ds(to, step)], sem.at[d2 * SIDE + d1]
                )
            )
    for copy in copies:
        copy.start()
    for copy in copies:
        copy.wait()


def place_blocks(table, parts):
    rows, n = parts[0].shape
    any_spec = pl.BlockSpec(memory_space=pl.ANY)
    return pl.pallas_call(
        place_blocks_kernel,
        out_shape=jax.ShapeDtypeStruct((SIDE * rows, n), parts[0].dtype),
        in_specs=[pl.BlockSpec(memory_space=pltpu.SMEM)] + [any_spec] * SIDE,
        out_specs=any_spec,
        scratch_shapes=[pltpu.SemaphoreType.DMA((SIDE * SIDE,))],
        cost_estimate=pl.CostEstimate(
            flops=0, bytes_accessed=16 * rows * n, transcendentals=0
        ),
        name="place_blocks",
    )(table, *parts)


def spread_phase1(a):
    got = [plane_shift(a, 0, d) for d in range(1, SIDE)]
    return jnp.concatenate([a] + got, axis=0)


def spread_phase2(a):
    return [a] + [plane_shift(a, 1, d) for d in range(1, SIDE)]


def total(parts):
    acc = parts[0].astype(WIDE)
    for p in parts[1:]:
        acc = acc + p.astype(WIDE)
    return acc


def gathered_sum(terms):
    got = [plane_shift(t, 1, -d) for d, t in enumerate(terms) if d]
    mine = total([terms[0]] + got).astype(HALF)
    step = mine.shape[0] // SIDE
    parts = [mine[d * step : (d + 1) * step] for d in range(SIDE)]
    got = [plane_shift(p, 0, -d) for d, p in enumerate(parts) if d]
    return total([parts[0]] + got)


def pair_and_others(own):
    other = core_swap(own)
    pair = (own.astype(WIDE) + other.astype(WIDE)).astype(HALF)
    return other, [pair] + [x_shift(pair, d) for d in range(1, SIDE)]


def masked_sum(first, parts, keep):
    acc = first
    for part, k in zip(parts, keep):
        acc = acc + jnp.where(k, part.astype(WIDE), 0.0)
    return acc


def on_device(tokens, w_query, w_key, w_value, w_out, grad_out, state_in):
    x, core = lax.axis_index("x"), lax.axis_index("core")
    dh = w_query.shape[1]
    rows = tokens.shape[0]
    table = block_table()

    t1 = spread_phase1(tokens.T)
    g1 = spread_phase1(grad_out.T)
    w_qkv, w_o = order_weights(table, w_query, w_key, w_value, w_out)
    t_parts = spread_phase2(t1)
    g_parts = spread_phase2(g1)
    step = t1.shape[0]
    wq_parts = [w_qkv[d * step : (d + 1) * step] for d in range(SIDE)]
    wo_parts = [w_o[d * step : (d + 1) * step] for d in range(SIDE)]

    qkv = sum(mm(t, w, TN) for t, w in zip(t_parts, wq_parts)).astype(HALF)
    query, keys, values = (qkv[:, i * dh : (i + 1) * dh] for i in range(3))

    own_state = mm(keys, values, TN).astype(HALF)
    other, pairs = pair_and_others(own_state)
    prior = masked_sum(
        state_in[0], [other] + pairs[1:], [core == 1] + [x >= d for d in range(1, SIDE)]
    ).astype(HALF)

    allowed = jnp.tril(jnp.ones((rows, rows), jnp.bool_))
    scores = jnp.where(allowed, mm(query, keys, NT), 0.0).astype(HALF)
    mixed = mm(scores, values, NN) + mm(query, prior, NN)
    inv_norm = lax.rsqrt(jnp.mean(mixed * mixed, axis=-1, keepdims=True) + EPSILON)
    normed = (mixed * inv_norm).astype(HALF)

    grad_normed = sum(mm(g, w, TN) for g, w in zip(g_parts, wo_parts))
    grad_mixed = inv_norm * (
        grad_normed
        - mixed * inv_norm * inv_norm * jnp.mean(grad_normed * mixed, axis=-1, keepdims=True)
    )
    grad_mixed = grad_mixed.astype(HALF)
    own_back = mm(query, grad_mixed, TN).astype(HALF)
    other_back, back_pairs = pair_and_others(own_back)
    later = masked_sum(
        jnp.zeros((dh, dh), WIDE),
        [other_back] + back_pairs[1:],
        [core == 0] + [x < d for d in range(1, SIDE)],
    ).astype(HALF)
    grad_state = jnp.zeros((dh, dh), WIDE)
    for chip in range(SIDE):
        part = jnp.zeros((dh, dh), HALF)
        for d, p in enumerate(back_pairs):
            part = jnp.where((x - d) % SIDE == chip, p, part)
        grad_state = grad_state + part.astype(WIDE)

    out_terms = [mm(w, normed, NT).astype(HALF) for w in wo_parts]
    result = gathered_sum(out_terms).astype(HALF).T

    grad_scores = jnp.where(allowed, mm(grad_mixed, values, NT), 0.0).astype(HALF)
    grad_query = (mm(grad_scores, keys, NN) + mm(grad_mixed, prior, NT)).astype(HALF)
    tokens_all = place_blocks(table, t_parts)
    grads_all = place_blocks(table, g_parts)
    early = jnp.concatenate(
        [mm(tokens_all, grad_query, NN).astype(HALF), mm(grads_all, normed, NN).astype(HALF)],
        axis=1,
    )
    early = lax.psum_scatter(early, SEQ, scatter_dimension=0, tiled=True)

    grad_keys = (mm(grad_scores, query, TN) + mm(values, later, NT)).astype(HALF)
    grad_values = (mm(scores, grad_mixed, TN) + mm(keys, later, NN)).astype(HALF)
    grad_kv = jnp.concatenate([grad_keys, grad_values], axis=1)
    late = mm(tokens_all, grad_kv, NN).astype(HALF)
    late = lax.psum_scatter(late, SEQ, scatter_dimension=0, tiled=True)

    grad_qkv = jnp.concatenate([grad_query, grad_kv], axis=1)
    in_terms = [mm(w, grad_qkv, NT).astype(HALF) for w in wq_parts]
    grad_tokens = gathered_sum(in_terms).T

    early, late = early.astype(WIDE), late.astype(WIDE)
    return (
        result,
        grad_tokens,
        early[:, :dh],
        late[:, :dh],
        late[:, dh:],
        early[:, dh:].T,
        grad_state[None],
    )


def solution(mesh):
    sizes = (SIDE, mesh.shape["seq"] // SIDE, SIDE, SIDE)
    torus = Mesh(mesh.devices.reshape(sizes), SEQ + HEAD)
    seq_head = P(SEQ, HEAD)
    column = P(None, HEAD)
    return jax.shard_map(
        on_device,
        mesh=torus,
        in_specs=(seq_head, column, column, column, P(HEAD, None), seq_head, P(HEAD, None, None)),
        out_specs=(
            seq_head,
            seq_head,
            seq_head,
            seq_head,
            seq_head,
            P(HEAD, SEQ),
            P(HEAD, None, None),
        ),
        check_vma=False,
    )
```

```python
import jax
import jax.numpy as jnp
from jax import lax
from jax.experimental import pallas as pl
from jax.experimental.pallas import tpu as pltpu
from jax.sharding import Mesh
from jax.sharding import PartitionSpec as P

SEQ = ("x", "core")
HEAD = ("y", "z")
PLANE = ("core", "y", "z")
SIDE = 4
EPSILON = 1e-06
WIDE = jnp.float32
HALF = jnp.bfloat16

NN = (((1,), (0,)), ((), ()))
NT = (((1,), (1,)), ((), ()))
TN = (((0,), (0,)), ((), ()))


def mm(a, b, dims):
    return lax.dot_general(a, b, dims, preferred_element_type=WIDE)


def plane_pairs(phase, shift):
    pairs = []
    for core in range(2):
        for y in range(SIDE):
            for z in range(SIDE):
                along_y = core == phase
                ty = (y + shift) % SIDE if along_y else y
                tz = z if along_y else (z + shift) % SIDE
                pairs.append(((core * SIDE + y) * SIDE + z, (core * SIDE + ty) * SIDE + tz))
    return pairs


def plane_shift(a, phase, shift):
    return lax.ppermute(a, PLANE, plane_pairs(phase, shift))


def x_shift(a, shift):
    return lax.ppermute(a, "x", [(i, (i + shift) % SIDE) for i in range(SIDE)])


def core_swap(a):
    return lax.ppermute(a, "core", [(0, 1), (1, 0)])


def block_tables():
    x, core, y, z = (lax.axis_index(n) for n in ("x",) + PLANE)
    at = jnp.arange(SIDE * SIDE, dtype=jnp.int32)
    d2, d1 = at // SIDE, at % SIDE
    from_y = (y - jnp.where(core == 0, d1, d2)) % SIDE
    from_z = (z - jnp.where(core == 0, d2, d1)) % SIDE
    other_core = (from_z // 2 + core) % 2
    slots = other_core * 8 + ((from_y - x) % SIDE) * 2 + from_z % 2
    return from_y * SIDE + from_z, slots


def order_weights_kernel(table, q, k, v, o, qkv_out, o_out):
    n = q.shape[1]
    step = q.shape[0] // (SIDE * SIDE)
    for i in range(SIDE * SIDE):
        at = pl.ds(pl.multiple_of(table[i] * step, step), step)
        to = slice(i * step, (i + 1) * step)
        qkv_out[to, :n] = q[at, :]
        qkv_out[to, n : 2 * n] = k[at, :]
        qkv_out[to, 2 * n :] = v[at, :]
        o_out[to, :] = o[:, at].T


def order_weights(table, w_query, w_key, w_value, w_out):
    rows, n = w_query.shape
    vmem = pl.BlockSpec(memory_space=pltpu.VMEM)
    return pl.pallas_call(
        order_weights_kernel,
        out_shape=(
            jax.ShapeDtypeStruct((rows, 3 * n), HALF),
            jax.ShapeDtypeStruct((rows, n), HALF),
        ),
        in_specs=[pl.BlockSpec(memory_space=pltpu.SMEM)] + [vmem] * 4,
        out_specs=(vmem, vmem),
        compiler_params=pltpu.CompilerParams(vmem_limit_bytes=24 << 20),
        cost_estimate=pl.CostEstimate(
            flops=0, bytes_accessed=16 * rows * n, transcendentals=0
        ),
        name="order_weights",
    )(table, w_query, w_key, w_value, w_out)


def weight_grads_kernel(slots, *refs):
    *ins, keep, send = refs
    groups = [ins[i : i + SIDE + 1] for i in range(0, len(ins), SIDE + 1)]
    step = ins[0].shape[0] // SIDE
    half = SIDE * SIDE // 2
    for d2 in range(SIDE):
        for d1 in range(SIDE):
            terms = [
                jnp.dot(
                    g[d2][d1 * step : (d1 + 1) * step, :], g[SIDE][...], preferred_element_type=WIDE
                ).astype(HALF)
                for g in groups
            ]
            slot = slots[d2 * SIDE + d1]

            @pl.when(slot < half)
            def _():
                at = 0
                for t in terms:
                    keep[slot, :, at : at + t.shape[1]] = t
                    at += t.shape[1]

            @pl.when(slot >= half)
            def _():
                at = 0
                for t in terms:
                    send[slot - half, :, at : at + t.shape[1]] = t
                    at += t.shape[1]


def weight_grads(slots, *groups):
    rows, tokens = groups[0][0][0].shape
    step = rows // SIDE
    n = sum(g.shape[1] for _, g in groups)
    vmem = pl.BlockSpec(memory_space=pltpu.VMEM)
    args = [a for parts, g in groups for a in (*parts, g)]
    half = jax.ShapeDtypeStruct((SIDE * SIDE // 2, step, n), HALF)
    return pl.pallas_call(
        weight_grads_kernel,
        out_shape=(half, half),
        in_specs=[pl.BlockSpec(memory_space=pltpu.SMEM)] + [vmem] * len(args),
        out_specs=(vmem, vmem),
        compiler_params=pltpu.CompilerParams(vmem_limit_bytes=24 << 20),
        cost_estimate=pl.CostEstimate(
            flops=2 * SIDE * rows * tokens * n,
            bytes_accessed=2 * SIDE * rows * (tokens * len(groups) + n),
            transcendentals=0,
        ),
        name="weight_grads",
    )(slots, *args)


def seq_sum(keep, send):
    mine = (keep.astype(WIDE) + core_swap(send).astype(WIDE)).astype(HALF)
    n = mine.shape[2]
    parts = [mine[2 * d : 2 * d + 2] for d in range(SIDE)]
    got = [x_shift(p, d) for d, p in enumerate(parts) if d]
    return total([parts[0]] + got).reshape(-1, n)


def spread_phase1(a):
    return [a] + [plane_shift(a, 0, d) for d in range(1, SIDE)]


def spread_phase2(a):
    return [a] + [plane_shift(a, 1, d) for d in range(1, SIDE)]


def total(parts):
    acc = parts[0].astype(WIDE)
    for p in parts[1:]:
        acc = acc + p.astype(WIDE)
    return acc


def fold_phase1(terms):
    return [terms[0]] + [plane_shift(t, 1, -d) for d, t in enumerate(terms) if d]


def fold_phase2(got):
    mine = total(got).astype(HALF)
    step = mine.shape[0] // SIDE
    parts = [mine[d * step : (d + 1) * step] for d in range(SIDE)]
    return [parts[0]] + [plane_shift(p, 0, -d) for d, p in enumerate(parts) if d]


def pair_and_others(own):
    other = core_swap(own)
    pair = (own.astype(WIDE) + other.astype(WIDE)).astype(HALF)
    return other, [pair] + [x_shift(pair, d) for d in range(1, SIDE)]


def masked_sum(first, parts, keep):
    acc = first
    for part, k in zip(parts, keep):
        acc = acc + jnp.where(k, part.astype(WIDE), 0.0)
    return acc


def on_device(tokens, w_query, w_key, w_value, w_out, grad_out, state_in):
    x, core = lax.axis_index("x"), lax.axis_index("core")
    dh = w_query.shape[1]
    rows = tokens.shape[0]
    table, slots = block_tables()

    t1 = spread_phase1(tokens.T)
    g1 = spread_phase1(grad_out.T)
    weights = order_weights(table, w_query, w_key, w_value, w_out)
    t1, g1, (w_qkv, w_o) = lax.optimization_barrier((t1, g1, weights))
    t_parts = spread_phase2(jnp.concatenate(t1, axis=0))
    t_parts, g1 = lax.optimization_barrier((t_parts, jnp.concatenate(g1, axis=0)))
    g_parts = spread_phase2(g1)
    step = g1.shape[0]
    wq_parts = [w_qkv[d * step : (d + 1) * step] for d in range(SIDE)]
    wo_parts = [w_o[d * step : (d + 1) * step] for d in range(SIDE)]

    qkv = sum(mm(t, w, TN) for t, w in zip(t_parts, wq_parts)).astype(HALF)
    query, keys, values = (qkv[:, i * dh : (i + 1) * dh] for i in range(3))

    own_state = mm(keys, values, TN).astype(HALF)
    other, pairs = pair_and_others(own_state)
    prior = masked_sum(
        state_in[0], [other] + pairs[1:], [core == 1] + [x >= d for d in range(1, SIDE)]
    ).astype(HALF)

    allowed = jnp.tril(jnp.ones((rows, rows), jnp.bool_))
    scores = jnp.where(allowed, mm(query, keys, NT), 0.0).astype(HALF)
    mixed = mm(scores, values, NN) + mm(query, prior, NN)
    inv_norm = lax.rsqrt(jnp.mean(mixed * mixed, axis=-1, keepdims=True) + EPSILON)
    normed = (mixed * inv_norm).astype(HALF)
    normed, g_parts = lax.optimization_barrier((normed, g_parts))

    grad_normed = sum(mm(g, w, TN) for g, w in zip(g_parts, wo_parts))
    grad_mixed = inv_norm * (
        grad_normed
        - mixed * inv_norm * inv_norm * jnp.mean(grad_normed * mixed, axis=-1, keepdims=True)
    )
    grad_mixed = grad_mixed.astype(HALF)
    own_back = mm(query, grad_mixed, TN).astype(HALF)
    other_back, back_pairs = pair_and_others(own_back)

    out_terms = [mm(w, normed, NT).astype(HALF) for w in wo_parts]
    out_got = fold_phase1(out_terms)

    grad_scores = jnp.where(allowed, mm(grad_mixed, values, NT), 0.0).astype(HALF)
    grad_query = (mm(grad_scores, keys, NN) + mm(grad_mixed, prior, NT)).astype(HALF)
    early = weight_grads(slots, (t_parts, grad_query), (g_parts, normed))

    later = masked_sum(
        jnp.zeros((dh, dh), WIDE),
        [other_back] + back_pairs[1:],
        [core == 0] + [x < d for d in range(1, SIDE)],
    ).astype(HALF)
    grad_state = jnp.zeros((dh, dh), WIDE)
    for chip in range(SIDE):
        part = jnp.zeros((dh, dh), HALF)
        for d, p in enumerate(back_pairs):
            part = jnp.where((x - d) % SIDE == chip, p, part)
        grad_state = grad_state + part.astype(WIDE)

    grad_keys = (mm(grad_scores, query, TN) + mm(values, later, NT)).astype(HALF)
    grad_values = (mm(scores, grad_mixed, TN) + mm(keys, later, NN)).astype(HALF)
    grad_qkv = jnp.concatenate([grad_query, grad_keys, grad_values], axis=1)
    grad_qkv, out_got = lax.optimization_barrier((grad_qkv, out_got))
    in_terms = [mm(w, grad_qkv, NT).astype(HALF) for w in wq_parts]
    in_got = fold_phase1(in_terms)
    result = total(fold_phase2(out_got)).astype(HALF).T
    late = weight_grads(slots, (t_parts, grad_qkv[:, dh:]))
    early = seq_sum(*early)
    late = seq_sum(*late)
    grad_tokens = total(fold_phase2(in_got)).T
    return (
        result,
        grad_tokens,
        early[:, :dh],
        late[:, :dh],
        late[:, dh:],
        early[:, dh:].T,
        grad_state[None],
    )


def solution(mesh):
    sizes = (SIDE, mesh.shape["seq"] // SIDE, SIDE, SIDE)
    torus = Mesh(mesh.devices.reshape(sizes), SEQ + HEAD)
    seq_head = P(SEQ, HEAD)
    column = P(None, HEAD)
    return jax.shard_map(
        on_device,
        mesh=torus,
        in_specs=(seq_head, column, column, column, P(HEAD, None), seq_head, P(HEAD, None, None)),
        out_specs=(
            seq_head,
            seq_head,
            seq_head,
            seq_head,
            seq_head,
            P(HEAD, SEQ),
            P(HEAD, None, None),
        ),
        check_vma=False,
    )
```

```python
import jax
import jax.numpy as jnp
from jax import lax
from jax.experimental import pallas as pl
from jax.experimental.pallas import tpu as pltpu
from jax.sharding import Mesh
from jax.sharding import PartitionSpec as P

SEQ = ("x", "core")
HEAD = ("y", "z")
PLANE = ("core", "y", "z")
SIDE = 4
EPSILON = 1e-06
WIDE = jnp.float32
HALF = jnp.bfloat16

NN = (((1,), (0,)), ((), ()))
NT = (((1,), (1,)), ((), ()))
TN = (((0,), (0,)), ((), ()))


def mm(a, b, dims):
    return lax.dot_general(a, b, dims, preferred_element_type=WIDE)


def after(first, then):
    return lax.optimization_barrier((first, then))[1]


def plane_pairs(phase, shift):
    pairs = []
    for core in range(2):
        for y in range(SIDE):
            for z in range(SIDE):
                along_y = core == phase
                ty = (y + shift) % SIDE if along_y else y
                tz = z if along_y else (z + shift) % SIDE
                pairs.append(((core * SIDE + y) * SIDE + z, (core * SIDE + ty) * SIDE + tz))
    return pairs


def plane_shift(a, phase, shift):
    return lax.ppermute(a, PLANE, plane_pairs(phase, shift))


def x_shift(a, shift):
    return lax.ppermute(a, "x", [(i, (i + shift) % SIDE) for i in range(SIDE)])


def x_outward(a):
    pairs = []
    for i in range(SIDE):
        pairs.append((2 * i, 2 * ((i + 1) % SIDE)))
        pairs.append((2 * i + 1, 2 * ((i - 1) % SIDE) + 1))
    return lax.ppermute(a, SEQ, pairs)


def core_swap(a):
    return lax.ppermute(a, "core", [(0, 1), (1, 0)])


def block_tables():
    core, y, z = (lax.axis_index(n) for n in PLANE)
    at = jnp.arange(SIDE * SIDE, dtype=jnp.int32)
    d2, d1 = at // SIDE, at % SIDE
    from_y = (y - jnp.where(core == 0, d1, d2)) % SIDE
    from_z = (z - jnp.where(core == 0, d2, d1)) % SIDE
    other_core = (from_z // 2 + core) % 2
    slots = other_core * 8 + from_y * 2 + from_z % 2
    return from_y * SIDE + from_z, slots


def order_weights_kernel(table, q, k, v, o, qkv_out, o_out):
    n = q.shape[1]
    step = q.shape[0] // (SIDE * SIDE)
    for i in range(SIDE * SIDE):
        at = pl.ds(pl.multiple_of(table[i] * step, step), step)
        to = slice(i * step, (i + 1) * step)
        qkv_out[to, :n] = q[at, :]
        qkv_out[to, n : 2 * n] = k[at, :]
        qkv_out[to, 2 * n :] = v[at, :]
        o_out[to, :] = o[:, at].T


def order_weights(table, w_query, w_key, w_value, w_out):
    rows, n = w_query.shape
    tall = pl.BlockSpec((rows, n), lambda i: (0, 0))
    return pl.pallas_call(
        order_weights_kernel,
        out_shape=(
            jax.ShapeDtypeStruct((rows, 3 * n), HALF),
            jax.ShapeDtypeStruct((rows, n), HALF),
        ),
        grid=(1,),
        in_specs=[pl.BlockSpec(memory_space=pltpu.SMEM), tall, tall, tall]
        + [pl.BlockSpec((n, rows), lambda i: (0, 0))],
        out_specs=(pl.BlockSpec((rows, 3 * n), lambda i: (0, 0)), tall),
        compiler_params=pltpu.CompilerParams(vmem_limit_bytes=18 << 20),
        cost_estimate=pl.CostEstimate(
            flops=0, bytes_accessed=16 * rows * n, transcendentals=0
        ),
        name="order_weights",
    )(table, w_query, w_key, w_value, w_out)


def sort_blocks_kernel(slots, a0, a1, a2, a3, out):
    step = a0.shape[0] // SIDE
    for d2, part in enumerate((a0, a1, a2, a3)):
        for d1 in range(SIDE):
            out[slots[d2 * SIDE + d1]] = part[d1 * step : (d1 + 1) * step, :]


def sort_blocks(slots, parts):
    rows, n = parts[0].shape
    shape = (SIDE * SIDE, rows // SIDE, n)
    return pl.pallas_call(
        sort_blocks_kernel,
        out_shape=jax.ShapeDtypeStruct(shape, HALF),
        grid=(1,),
        in_specs=[pl.BlockSpec(memory_space=pltpu.SMEM)]
        + [pl.BlockSpec((rows, n), lambda i: (0, 0))] * SIDE,
        out_specs=pl.BlockSpec(shape, lambda i: (0, 0, 0)),
        compiler_params=pltpu.CompilerParams(vmem_limit_bytes=9 << 20),
        cost_estimate=pl.CostEstimate(
            flops=0, bytes_accessed=16 * rows * n, transcendentals=0
        ),
        name="sort_blocks",
    )(slots, *parts)


def weight_grads_kernel(t_own, t_other, g_own, g_other, d_own, d_other, out):
    n = d_own.shape[1]
    split = n - n // SIDE
    for s in range(t_own.shape[0]):
        for own, other, at in ((t_own, t_other, slice(0, split)), (g_own, g_other, slice(split, n))):
            term = jnp.dot(own[s], d_own[:, at], preferred_element_type=WIDE)
            term = term + jnp.dot(other[s], d_other[:, at], preferred_element_type=WIDE)
            out[s, :, at] = term.astype(HALF)


def weight_grads(t_sorted, t_other, g_sorted, g_other, d_own, d_other):
    half, step, tokens = t_other.shape
    n = d_own.shape[1]
    first = pl.BlockSpec((half, step, tokens), lambda i: (0, 0, 0))
    flat = pl.BlockSpec((tokens, n), lambda i: (0, 0))
    return pl.pallas_call(
        weight_grads_kernel,
        out_shape=jax.ShapeDtypeStruct((half, step, n), HALF),
        grid=(1,),
        in_specs=[first] * 4 + [flat] * 2,
        out_specs=pl.BlockSpec((half, step, n), lambda i: (0, 0, 0)),
        compiler_params=pltpu.CompilerParams(vmem_limit_bytes=14 << 20),
        cost_estimate=pl.CostEstimate(
            flops=4 * half * step * tokens * n,
            bytes_accessed=2 * half * step * (4 * tokens + n),
            transcendentals=0,
        ),
        name="weight_grads",
    )(t_sorted, t_other, g_sorted, g_other, d_own, d_other)


def part_terms_kernel(w, cotangent, out):
    step = w.shape[0] // SIDE
    for i in range(SIDE):
        at = slice(i * step, (i + 1) * step)
        out[at, :] = mm(cotangent[...], w[at, :], NT).astype(HALF)


def part_terms(weights, part, cotangent):
    rows, n = weights.shape
    rows = rows // SIDE
    tokens = cotangent.shape[0]
    return pl.pallas_call(
        part_terms_kernel,
        out_shape=jax.ShapeDtypeStruct((SIDE * tokens, rows // SIDE), HALF),
        grid=(1,),
        in_specs=[
            pl.BlockSpec((rows, n), lambda i: (part, 0)),
            pl.BlockSpec((tokens, n), lambda i: (0, 0)),
        ],
        out_specs=pl.BlockSpec((SIDE * tokens, rows // SIDE), lambda i: (0, 0)),
        compiler_params=pltpu.CompilerParams(vmem_limit_bytes=4 << 20),
        cost_estimate=pl.CostEstimate(
            flops=2 * rows * n * tokens, bytes_accessed=2 * rows * (n + tokens), transcendentals=0
        ),
        name="part_terms",
    )(weights, cotangent)


def x_spread(blocks):
    _, step, n = blocks.shape
    return lax.all_to_all(blocks.reshape(SIDE, 2 * step, n), "x", 0, 0, tiled=True)


def split_sum_kernel(got, q, k, v, o):
    n = q.shape[1]
    for i, out in enumerate((q, k, v, o)):
        at = slice(i * n, (i + 1) * n)
        acc = got[0, :, at].astype(WIDE)
        for d in range(1, SIDE):
            acc = acc + got[d, :, at].astype(WIDE)
        out[...] = acc if out is not o else acc.T


def split_sum(got):
    _, rows, width = got.shape
    n = width // SIDE
    flat = pl.BlockSpec((rows, n), lambda i: (0, 0))
    tall = jax.ShapeDtypeStruct((rows, n), WIDE)
    return pl.pallas_call(
        split_sum_kernel,
        out_shape=(tall, tall, tall, jax.ShapeDtypeStruct((n, rows), WIDE)),
        grid=(1,),
        in_specs=[pl.BlockSpec(got.shape, lambda i: (0, 0, 0))],
        out_specs=(flat, flat, flat, pl.BlockSpec((n, rows), lambda i: (0, 0))),
        compiler_params=pltpu.CompilerParams(vmem_limit_bytes=7 << 20),
        cost_estimate=pl.CostEstimate(
            flops=SIDE * rows * width, bytes_accessed=12 * rows * width, transcendentals=0
        ),
        name="split_sum",
    )(got)


def spread_phase1(a):
    return [a] + [plane_shift(a, 0, d) for d in range(1, SIDE)]


def spread_phase2(a):
    return [a] + [plane_shift(a, 1, d) for d in range(1, SIDE)]


def total(parts):
    acc = parts[0].astype(WIDE)
    for p in parts[1:]:
        acc = acc + p.astype(WIDE)
    return acc


def fold_phase1(terms):
    return [terms[0]] + [plane_shift(t, 1, -d) for d, t in enumerate(terms) if d]


def fold_phase2(mine):
    step = mine[0].shape[0] // SIDE
    parts = [jnp.stack([m[d * step : (d + 1) * step] for m in mine]) for d in range(SIDE)]
    return [parts[0]] + [plane_shift(p, 0, -d) for d, p in enumerate(parts) if d]


def pair_sums(own, other):
    core = lax.axis_index("core")
    pair = (own.astype(WIDE) + other.astype(WIDE)).astype(HALF)
    near, far = lax.optimization_barrier((x_outward(pair), x_shift(pair, 2)))
    across = core_swap(near)
    return [
        pair,
        jnp.where(core == 0, near, across),
        far,
        jnp.where(core == 0, across, near),
    ]


def masked_sum(first, parts, keep):
    acc = first
    for part, k in zip(parts, keep):
        acc = acc + jnp.where(k, part.astype(WIDE), 0.0)
    return acc


def on_device(tokens, w_query, w_key, w_value, w_out, grad_out, state_in):
    x, core = lax.axis_index("x"), lax.axis_index("core")
    dh = w_query.shape[1]
    rows = tokens.shape[0]
    table, slots = block_tables()

    t1 = jnp.concatenate(spread_phase1(tokens.T), axis=0)
    g1 = jnp.concatenate(spread_phase1(grad_out.T), axis=0)
    t1, raw = lax.optimization_barrier((t1, (w_query, w_key, w_value, w_out)))
    t_parts = spread_phase2(t1)
    w_qkv, w_o = order_weights(table, *raw)
    g_parts = spread_phase2(g1)
    step = g1.shape[0]
    wq_parts = [w_qkv[d * step : (d + 1) * step] for d in range(SIDE)]
    wo_parts = [w_o[d * step : (d + 1) * step] for d in range(SIDE)]

    qkv = sum(mm(t, w, TN) for t, w in zip(t_parts, wq_parts)).astype(HALF)
    query, keys, values = (qkv[:, i * dh : (i + 1) * dh] for i in range(3))

    own_state = mm(keys, values, TN).astype(HALF)
    other = core_swap(own_state)
    g_parts = after(other, g_parts)
    pairs = pair_sums(own_state, other)
    prior = masked_sum(
        state_in[0], [other] + pairs[1:], [core == 1] + [x >= d for d in range(1, SIDE)]
    ).astype(HALF)

    allowed = jnp.tril(jnp.ones((rows, rows), jnp.bool_))
    scores = jnp.where(allowed, mm(query, keys, NT), 0.0).astype(HALF)
    mixed = mm(scores, values, NN) + mm(query, prior, NN)
    inv_norm = lax.rsqrt(jnp.mean(mixed * mixed, axis=-1, keepdims=True) + EPSILON)
    normed = (mixed * inv_norm).astype(HALF)
    out_terms = [part_terms(w_o, d, normed) for d in range(SIDE)]
    out_got = fold_phase1(out_terms)

    grad_normed = sum(mm(g, w, TN) for g, w in zip(g_parts, wo_parts))
    grad_mixed = inv_norm * (
        grad_normed
        - mixed * inv_norm * inv_norm * jnp.mean(grad_normed * mixed, axis=-1, keepdims=True)
    )
    grad_mixed = grad_mixed.astype(HALF)
    own_back = mm(query, grad_mixed, TN).astype(HALF)
    half = SIDE * SIDE // 2
    t_sorted, g_sorted = sort_blocks(slots, t_parts), sort_blocks(slots, g_parts)
    t_other, g_other = (core_swap(after(prior, a[half:])) for a in (t_sorted, g_sorted))
    own_back = after((t_other, g_other), own_back)
    other_back = core_swap(own_back)
    back_pairs = pair_sums(own_back, other_back)

    grad_scores = jnp.where(allowed, mm(grad_mixed, values, NT), 0.0).astype(HALF)
    grad_query = (mm(grad_scores, keys, NN) + mm(grad_mixed, prior, NT)).astype(HALF)
    later = masked_sum(
        jnp.zeros((dh, dh), WIDE),
        [other_back] + back_pairs[1:],
        [core == 0] + [x < d for d in range(1, SIDE)],
    ).astype(HALF)
    grad_state = jnp.zeros((dh, dh), WIDE)
    for chip in range(SIDE):
        part = jnp.zeros((dh, dh), HALF)
        for d, p in enumerate(back_pairs):
            part = jnp.where((x - d) % SIDE == chip, p, part)
        grad_state = grad_state + part.astype(WIDE)

    grad_keys = (mm(grad_scores, query, TN) + mm(values, later, NT)).astype(HALF)
    grad_values = (mm(scores, grad_mixed, TN) + mm(keys, later, NN)).astype(HALF)
    cotangents = jnp.concatenate([grad_query, grad_keys, grad_values, normed], axis=1)
    blocks = weight_grads(
        t_sorted, t_other, g_sorted, g_other, cotangents, core_swap(cotangents)
    )
    out_sum = total(out_got).astype(HALF)
    cotangents, out_sum, blocks = lax.optimization_barrier((cotangents, out_sum, blocks))
    in_terms = [part_terms(w_qkv, d, cotangents) for d in range(SIDE)]
    in_got = fold_phase1(in_terms)
    grads = split_sum(x_spread(after(in_terms, blocks)))
    got = fold_phase2((out_sum, total(in_got).astype(HALF)))
    sums = total(after(grads, got))
    result, grad_tokens = sums[0].astype(HALF), sums[1]
    return (
        result,
        grad_tokens,
        *grads,
        grad_state[None],
    )


def solution(mesh):
    sizes = (SIDE, mesh.shape["seq"] // SIDE, SIDE, SIDE)
    torus = Mesh(mesh.devices.reshape(sizes), SEQ + HEAD)
    seq_head = P(SEQ, HEAD)
    column = P(None, HEAD)
    return jax.shard_map(
        on_device,
        mesh=torus,
        in_specs=(seq_head, column, column, column, P(HEAD, None), seq_head, P(HEAD, None, None)),
        out_specs=(
            seq_head,
            seq_head,
            seq_head,
            seq_head,
            seq_head,
            P(HEAD, SEQ),
            P(HEAD, None, None),
        ),
        check_vma=False,
    )
```

```python
import jax
import jax.numpy as jnp
from jax import lax
from jax.experimental import pallas as pl
from jax.experimental.pallas import tpu as pltpu
from jax.sharding import Mesh
from jax.sharding import PartitionSpec as P

SEQ = ("x", "core")
HEAD = ("y", "z")
PLANE = ("core", "y", "z")
SIDE = 4
EPSILON = 1e-06
WIDE = jnp.float32
HALF = jnp.bfloat16

NN = (((1,), (0,)), ((), ()))
NT = (((1,), (1,)), ((), ()))
TN = (((0,), (0,)), ((), ()))


def mm(a, b, dims):
    return lax.dot_general(a, b, dims, preferred_element_type=WIDE)


def after(first, then):
    return lax.optimization_barrier((first, then))[1]


def plane_pairs(phase, shift):
    pairs = []
    for core in range(2):
        for y in range(SIDE):
            for z in range(SIDE):
                along_y = core == phase
                ty = (y + shift) % SIDE if along_y else y
                tz = z if along_y else (z + shift) % SIDE
                pairs.append(((core * SIDE + y) * SIDE + z, (core * SIDE + ty) * SIDE + tz))
    return pairs


def plane_shift(a, phase, shift):
    return lax.ppermute(a, PLANE, plane_pairs(phase, shift))


def x_shift(a, shift):
    return lax.ppermute(a, "x", [(i, (i + shift) % SIDE) for i in range(SIDE)])


def x_outward(a):
    pairs = []
    for i in range(SIDE):
        pairs.append((2 * i, 2 * ((i + 1) % SIDE)))
        pairs.append((2 * i + 1, 2 * ((i - 1) % SIDE) + 1))
    return lax.ppermute(a, SEQ, pairs)


def x_partner(a, bits):
    pairs = [(2 * i + c, 2 * (i ^ bits[c]) + c) for i in range(SIDE) for c in range(2)]
    return lax.ppermute(a, SEQ, pairs)


def core_swap(a):
    return lax.ppermute(a, "core", [(0, 1), (1, 0)])


def block_tables():
    x, core, y, z = (lax.axis_index(n) for n in ("x",) + PLANE)
    at = jnp.arange(SIDE * SIDE, dtype=jnp.int32)
    d2, d1 = at // SIDE, at % SIDE
    from_y = (y - jnp.where(core == 0, d1, d2)) % SIDE
    from_z = (z - jnp.where(core == 0, d2, d1)) % SIDE
    other_core = (from_z // 2 + core) % 2
    away = x ^ from_y
    place = jnp.where(away % 2 == 0, away // 2, 2 + ((away // 2) ^ (from_z // 2)))
    slots = other_core * 8 + place * 2 + from_z % 2
    return from_y * SIDE + from_z, slots


def order_weights_kernel(table, q, k, v, o, qkv_out, o_out):
    n = q.shape[1]
    step = q.shape[0] // (SIDE * SIDE)
    for i in range(SIDE * SIDE):
        at = pl.ds(pl.multiple_of(table[i] * step, step), step)
        to = slice(i * step, (i + 1) * step)
        qkv_out[to, :n] = q[at, :]
        qkv_out[to, n : 2 * n] = k[at, :]
        qkv_out[to, 2 * n :] = v[at, :]
        o_out[to, :] = o[:, at].T


def order_weights(table, w_query, w_key, w_value, w_out):
    rows, n = w_query.shape
    tall = pl.BlockSpec((rows, n), lambda i: (0, 0))
    return pl.pallas_call(
        order_weights_kernel,
        out_shape=(
            jax.ShapeDtypeStruct((rows, 3 * n), HALF),
            jax.ShapeDtypeStruct((rows, n), HALF),
        ),
        grid=(1,),
        in_specs=[pl.BlockSpec(memory_space=pltpu.SMEM), tall, tall, tall]
        + [pl.BlockSpec((n, rows), lambda i: (0, 0))],
        out_specs=(pl.BlockSpec((rows, 3 * n), lambda i: (0, 0)), tall),
        compiler_params=pltpu.CompilerParams(vmem_limit_bytes=18 << 20),
        cost_estimate=pl.CostEstimate(
            flops=0, bytes_accessed=16 * rows * n, transcendentals=0
        ),
        name="order_weights",
    )(table, w_query, w_key, w_value, w_out)


def sort_blocks_kernel(slots, a0, a1, a2, a3, out):
    step = a0.shape[0] // SIDE
    for d2, part in enumerate((a0, a1, a2, a3)):
        for d1 in range(SIDE):
            out[slots[d2 * SIDE + d1]] = part[d1 * step : (d1 + 1) * step, :]


def sort_blocks(slots, parts):
    rows, n = parts[0].shape
    shape = (SIDE * SIDE, rows // SIDE, n)
    return pl.pallas_call(
        sort_blocks_kernel,
        out_shape=jax.ShapeDtypeStruct(shape, HALF),
        grid=(1,),
        in_specs=[pl.BlockSpec(memory_space=pltpu.SMEM)]
        + [pl.BlockSpec((rows, n), lambda i: (0, 0))] * SIDE,
        out_specs=pl.BlockSpec(shape, lambda i: (0, 0, 0)),
        compiler_params=pltpu.CompilerParams(vmem_limit_bytes=9 << 20),
        cost_estimate=pl.CostEstimate(
            flops=0, bytes_accessed=16 * rows * n, transcendentals=0
        ),
        name="sort_blocks",
    )(slots, *parts)


def weight_grads_kernel(t_own, t_other, g_own, g_other, d_own, d_other, keep, send):
    n = d_own.shape[1]
    half = keep.shape[0]
    split = n - n // SIDE
    for s in range(t_own.shape[0]):
        for own, other, at in ((t_own, t_other, slice(0, split)), (g_own, g_other, slice(split, n))):
            term = jnp.dot(own[s], d_own[:, at], preferred_element_type=WIDE)
            term = term + jnp.dot(other[s], d_other[:, at], preferred_element_type=WIDE)
            if s < half:
                keep[s, :, at] = term.astype(HALF)
            else:
                send[s - half, :, at] = term.astype(HALF)


def weight_grads(t_sorted, t_other, g_sorted, g_other, d_own, d_other):
    half, step, tokens = t_other.shape
    n = d_own.shape[1]
    first = pl.BlockSpec((half, step, tokens), lambda i: (0, 0, 0))
    flat = pl.BlockSpec((tokens, n), lambda i: (0, 0))
    return pl.pallas_call(
        weight_grads_kernel,
        out_shape=[jax.ShapeDtypeStruct((half // 2, step, n), HALF)] * 2,
        grid=(1,),
        in_specs=[first] * 4 + [flat] * 2,
        out_specs=[pl.BlockSpec((half // 2, step, n), lambda i: (0, 0, 0))] * 2,
        compiler_params=pltpu.CompilerParams(vmem_limit_bytes=14 << 20),
        cost_estimate=pl.CostEstimate(
            flops=4 * half * step * tokens * n,
            bytes_accessed=2 * half * step * (4 * tokens + n),
            transcendentals=0,
        ),
        name="weight_grads",
    )(t_sorted, t_other, g_sorted, g_other, d_own, d_other)


def part_terms_kernel(w, cotangent, out):
    step = w.shape[0] // SIDE
    for i in range(SIDE):
        at = slice(i * step, (i + 1) * step)
        out[at, :] = mm(cotangent[...], w[at, :], NT).astype(HALF)


def part_terms(weights, part, cotangent):
    rows, n = weights.shape
    rows = rows // SIDE
    tokens = cotangent.shape[0]
    return pl.pallas_call(
        part_terms_kernel,
        out_shape=jax.ShapeDtypeStruct((SIDE * tokens, rows // SIDE), HALF),
        grid=(1,),
        in_specs=[
            pl.BlockSpec((rows, n), lambda i: (part, 0)),
            pl.BlockSpec((tokens, n), lambda i: (0, 0)),
        ],
        out_specs=pl.BlockSpec((SIDE * tokens, rows // SIDE), lambda i: (0, 0)),
        compiler_params=pltpu.CompilerParams(vmem_limit_bytes=4 << 20),
        cost_estimate=pl.CostEstimate(
            flops=2 * rows * n * tokens, bytes_accessed=2 * rows * (n + tokens), transcendentals=0
        ),
        name="part_terms",
    )(weights, cotangent)


def split_sum_kernel(mine, got, q, k, v, o):
    n = q.shape[1]
    for i, out in enumerate((q, k, v, o)):
        at = slice(i * n, (i + 1) * n)
        acc = mine[:, at].astype(WIDE) + got[:, at].astype(WIDE)
        out[...] = acc if out is not o else acc.T


def split_sum(mine, got):
    rows, width = got.shape
    n = width // SIDE
    flat = pl.BlockSpec((rows, n), lambda i: (0, 0))
    tall = jax.ShapeDtypeStruct((rows, n), WIDE)
    return pl.pallas_call(
        split_sum_kernel,
        out_shape=(tall, tall, tall, jax.ShapeDtypeStruct((n, rows), WIDE)),
        grid=(1,),
        in_specs=[pl.BlockSpec((rows, width), lambda i: (0, 0))] * 2,
        out_specs=(flat, flat, flat, pl.BlockSpec((n, rows), lambda i: (0, 0))),
        compiler_params=pltpu.CompilerParams(vmem_limit_bytes=5 << 20),
        cost_estimate=pl.CostEstimate(
            flops=rows * width, bytes_accessed=8 * rows * width, transcendentals=0
        ),
        name="split_sum",
    )(mine, got)


def spread_phase1(a):
    return [a] + [plane_shift(a, 0, d) for d in range(1, SIDE)]


def spread_phase2(a):
    return [a] + [plane_shift(a, 1, d) for d in range(1, SIDE)]


def total(parts):
    acc = parts[0].astype(WIDE)
    for p in parts[1:]:
        acc = acc + p.astype(WIDE)
    return acc


def fold_phase1(terms):
    return [terms[0]] + [plane_shift(t, 1, -d) for d, t in enumerate(terms) if d]


def fold_phase2(mine):
    step = mine[0].shape[0] // SIDE
    parts = [jnp.stack([m[d * step : (d + 1) * step] for m in mine]) for d in range(SIDE)]
    return [parts[0]] + [plane_shift(p, 0, -d) for d, p in enumerate(parts) if d]


def pair_sums(own, other):
    core = lax.axis_index("core")
    pair = (own.astype(WIDE) + other.astype(WIDE)).astype(HALF)
    near, far = lax.optimization_barrier((x_outward(pair), x_shift(pair, 2)))
    across = core_swap(near)
    return [
        pair,
        jnp.where(core == 0, near, across),
        far,
        jnp.where(core == 0, across, near),
    ]


def masked_sum(first, parts, keep):
    acc = first
    for part, k in zip(parts, keep):
        acc = acc + jnp.where(k, part.astype(WIDE), 0.0)
    return acc


def rounded_sum(a, b):
    return (a.astype(WIDE) + b.astype(WIDE)).astype(HALF)


def seq_exchange(own, earlier):
    x, core = lax.axis_index("x"), lax.axis_index("core")
    other = core_swap(own)
    pair = rounded_sum(own, other)
    near = x_partner(pair, (1, 1))
    four = rounded_sum(pair, near)
    far = x_partner(four, (2, 2))
    ahead = [core == 1, x % 2 == 1, x >= 2]
    acc = jnp.zeros(own.shape, WIDE)
    for part, before in zip((other, near, far), ahead):
        keep = before if earlier else jnp.logical_not(before)
        acc = acc + jnp.where(keep, part.astype(WIDE), 0.0)
    return acc, (four, far), other


def on_device(tokens, w_query, w_key, w_value, w_out, grad_out, state_in):
    x, core = lax.axis_index("x"), lax.axis_index("core")
    dh = w_query.shape[1]
    rows = tokens.shape[0]
    table, slots = block_tables()

    t1 = jnp.concatenate(spread_phase1(tokens.T), axis=0)
    g1 = jnp.concatenate(spread_phase1(grad_out.T), axis=0)
    t1, raw = lax.optimization_barrier((t1, (w_query, w_key, w_value, w_out)))
    t_parts = spread_phase2(t1)
    w_qkv, w_o = order_weights(table, *raw)
    g_parts = spread_phase2(g1)
    step = g1.shape[0]
    wq_parts = [w_qkv[d * step : (d + 1) * step] for d in range(SIDE)]
    wo_parts = [w_o[d * step : (d + 1) * step] for d in range(SIDE)]

    qkv = sum(mm(t, w, TN) for t, w in zip(t_parts, wq_parts)).astype(HALF)
    query, keys, values = (qkv[:, i * dh : (i + 1) * dh] for i in range(3))

    own_state = mm(keys, values, TN).astype(HALF)
    other = core_swap(own_state)
    g_parts = after(other, g_parts)
    pairs = pair_sums(own_state, other)
    prior = masked_sum(
        state_in[0], [other] + pairs[1:], [core == 1] + [x >= d for d in range(1, SIDE)]
    ).astype(HALF)

    allowed = jnp.tril(jnp.ones((rows, rows), jnp.bool_))
    scores = jnp.where(allowed, mm(query, keys, NT), 0.0).astype(HALF)
    mixed = mm(scores, values, NN) + mm(query, prior, NN)
    inv_norm = lax.rsqrt(jnp.mean(mixed * mixed, axis=-1, keepdims=True) + EPSILON)
    normed = (mixed * inv_norm).astype(HALF)
    out_terms = [part_terms(w_o, d, normed) for d in range(SIDE)]
    out_got = fold_phase1(out_terms)

    grad_normed = sum(mm(g, w, TN) for g, w in zip(g_parts, wo_parts))
    grad_mixed = inv_norm * (
        grad_normed
        - mixed * inv_norm * inv_norm * jnp.mean(grad_normed * mixed, axis=-1, keepdims=True)
    )
    grad_mixed = grad_mixed.astype(HALF)
    own_back = mm(query, grad_mixed, TN).astype(HALF)
    half = SIDE * SIDE // 2
    t_sorted, g_sorted = sort_blocks(slots, t_parts), sort_blocks(slots, g_parts)
    own_back = after(out_terms, own_back)
    behind, halves, _ = seq_exchange(own_back, False)
    t_other, g_other = (core_swap(after(halves[0], a[half:])) for a in (t_sorted, g_sorted))

    grad_scores = jnp.where(allowed, mm(grad_mixed, values, NT), 0.0).astype(HALF)
    grad_query = (mm(grad_scores, keys, NN) + mm(grad_mixed, prior, NT)).astype(HALF)
    later = behind.astype(HALF)
    grad_state = total(halves)
    grad_keys = (mm(grad_scores, query, TN) + mm(values, later, NT)).astype(HALF)
    grad_values = (mm(scores, grad_mixed, TN) + mm(keys, later, NN)).astype(HALF)
    out_sum = total(out_got).astype(HALF)
    cotangents = jnp.concatenate([grad_query, grad_keys, grad_values, normed], axis=1)
    cotangents, out_sum = lax.optimization_barrier((cotangents, out_sum))
    keep, send = weight_grads(
        t_sorted, t_other, g_sorted, g_other, cotangents, core_swap(cotangents)
    )
    sent = x_partner(send, (1, 3))
    in_terms = [part_terms(w_qkv, d, cotangents) for d in range(SIDE)]
    in_got = fold_phase1(in_terms)
    mine = (keep.astype(WIDE) + sent.astype(WIDE)).astype(HALF)
    mine = mine.reshape(2, -1, mine.shape[2])
    own, send = mine[0], mine[1]
    in_got = after((own, send), in_got)
    grads = split_sum(own, x_partner(send, (2, 2)))
    got = fold_phase2((out_sum, total(in_got).astype(HALF)))
    got = after(grads, got)
    result = total([g[0] for g in got]).astype(HALF)
    grad_tokens = total([g[1] for g in got])
    return (
        result,
        grad_tokens,
        *grads,
        grad_state[None],
    )


def solution(mesh):
    sizes = (SIDE, mesh.shape["seq"] // SIDE, SIDE, SIDE)
    torus = Mesh(mesh.devices.reshape(sizes), SEQ + HEAD)
    seq_head = P(SEQ, HEAD)
    column = P(None, HEAD)
    return jax.shard_map(
        on_device,
        mesh=torus,
        in_specs=(seq_head, column, column, column, P(HEAD, None), seq_head, P(HEAD, None, None)),
        out_specs=(
            seq_head,
            seq_head,
            seq_head,
            seq_head,
            seq_head,
            P(HEAD, SEQ),
            P(HEAD, None, None),
        ),
        check_vma=False,
    )
```

```python
import jax
import jax.numpy as jnp
from jax import lax
from jax.experimental import pallas as pl
from jax.experimental.pallas import tpu as pltpu
from jax.sharding import Mesh
from jax.sharding import PartitionSpec as P

SEQ = ("x", "core")
HEAD = ("y", "z")
PLANE = ("core", "y", "z")
SIDE = 4
EPSILON = 1e-06
WIDE = jnp.float32
HALF = jnp.bfloat16

NN = (((1,), (0,)), ((), ()))
NT = (((1,), (1,)), ((), ()))
TN = (((0,), (0,)), ((), ()))


def mm(a, b, dims):
    return lax.dot_general(a, b, dims, preferred_element_type=WIDE)


def after(first, then):
    return lax.optimization_barrier((first, then))[1]


def plane_pairs(phase, shift):
    pairs = []
    for core in range(2):
        for y in range(SIDE):
            for z in range(SIDE):
                along_y = core == phase
                ty = (y + shift) % SIDE if along_y else y
                tz = z if along_y else (z + shift) % SIDE
                pairs.append(((core * SIDE + y) * SIDE + z, (core * SIDE + ty) * SIDE + tz))
    return pairs


def plane_shift(a, phase, shift):
    return lax.ppermute(a, PLANE, plane_pairs(phase, shift))


def x_shift(a, shift):
    return lax.ppermute(a, "x", [(i, (i + shift) % SIDE) for i in range(SIDE)])


def x_outward(a):
    pairs = []
    for i in range(SIDE):
        pairs.append((2 * i, 2 * ((i + 1) % SIDE)))
        pairs.append((2 * i + 1, 2 * ((i - 1) % SIDE) + 1))
    return lax.ppermute(a, SEQ, pairs)


def x_partner(a, bits):
    pairs = [(2 * i + c, 2 * (i ^ bits[c]) + c) for i in range(SIDE) for c in range(2)]
    return lax.ppermute(a, SEQ, pairs)


def core_swap(a):
    return lax.ppermute(a, "core", [(0, 1), (1, 0)])


def block_tables():
    x, core, y, z = (lax.axis_index(n) for n in ("x",) + PLANE)
    at = jnp.arange(SIDE * SIDE, dtype=jnp.int32)
    d2, d1 = at // SIDE, at % SIDE
    from_y = (y - jnp.where(core == 0, d1, d2)) % SIDE
    from_z = (z - jnp.where(core == 0, d2, d1)) % SIDE
    other_core = (from_z // 2 + core) % 2
    away = x ^ from_y
    place = jnp.where(away % 2 == 0, away // 2, 2 + ((away // 2) ^ (from_z // 2)))
    slots = other_core * 8 + place * 2 + from_z % 2
    return from_y * SIDE + from_z, slots


def order_weights_kernel(table, q, k, v, o, qkv_out, o_out):
    n = q.shape[1]
    step = q.shape[0] // (SIDE * SIDE)
    for i in range(SIDE * SIDE):
        at = pl.ds(pl.multiple_of(table[i] * step, step), step)
        to = slice(i * step, (i + 1) * step)
        qkv_out[to, :n] = q[at, :]
        qkv_out[to, n : 2 * n] = k[at, :]
        qkv_out[to, 2 * n :] = v[at, :]
        o_out[to, :] = o[:, at].T


def order_weights(table, w_query, w_key, w_value, w_out):
    rows, n = w_query.shape
    tall = pl.BlockSpec((rows, n), lambda i: (0, 0))
    return pl.pallas_call(
        order_weights_kernel,
        out_shape=(
            jax.ShapeDtypeStruct((rows, 3 * n), HALF),
            jax.ShapeDtypeStruct((rows, n), HALF),
        ),
        grid=(1,),
        in_specs=[pl.BlockSpec(memory_space=pltpu.SMEM), tall, tall, tall]
        + [pl.BlockSpec((n, rows), lambda i: (0, 0))],
        out_specs=(pl.BlockSpec((rows, 3 * n), lambda i: (0, 0)), tall),
        compiler_params=pltpu.CompilerParams(vmem_limit_bytes=18 << 20),
        cost_estimate=pl.CostEstimate(
            flops=0, bytes_accessed=16 * rows * n, transcendentals=0
        ),
        name="order_weights",
    )(table, w_query, w_key, w_value, w_out)


def sort_blocks_kernel(slots, a0, a1, a2, a3, out):
    step = a0.shape[0] // SIDE
    for d2, part in enumerate((a0, a1, a2, a3)):
        for d1 in range(SIDE):
            out[slots[d2 * SIDE + d1]] = part[d1 * step : (d1 + 1) * step, :]


def sort_blocks(slots, parts):
    rows, n = parts[0].shape
    shape = (SIDE * SIDE, rows // SIDE, n)
    return pl.pallas_call(
        sort_blocks_kernel,
        out_shape=jax.ShapeDtypeStruct(shape, HALF),
        grid=(1,),
        in_specs=[pl.BlockSpec(memory_space=pltpu.SMEM)]
        + [pl.BlockSpec((rows, n), lambda i: (0, 0))] * SIDE,
        out_specs=pl.BlockSpec(shape, lambda i: (0, 0, 0)),
        compiler_params=pltpu.CompilerParams(vmem_limit_bytes=9 << 20),
        cost_estimate=pl.CostEstimate(
            flops=0, bytes_accessed=16 * rows * n, transcendentals=0
        ),
        name="sort_blocks",
    )(slots, *parts)


def weight_grads_kernel(t_own, t_other, g_own, g_other, d_own, d_other, keep, send):
    n = d_own.shape[1]
    half = keep.shape[0]
    split = n - n // SIDE
    for s in range(t_own.shape[0]):
        for own, other, at in ((t_own, t_other, slice(0, split)), (g_own, g_other, slice(split, n))):
            term = jnp.dot(own[s], d_own[:, at], preferred_element_type=WIDE)
            term = term + jnp.dot(other[s], d_other[:, at], preferred_element_type=WIDE)
            if s < half:
                keep[s, :, at] = term.astype(HALF)
            else:
                send[s - half, :, at] = term.astype(HALF)


def weight_grads(t_sorted, t_other, g_sorted, g_other, d_own, d_other):
    half, step, tokens = t_other.shape
    n = d_own.shape[1]
    first = pl.BlockSpec((half, step, tokens), lambda i: (0, 0, 0))
    flat = pl.BlockSpec((tokens, n), lambda i: (0, 0))
    return pl.pallas_call(
        weight_grads_kernel,
        out_shape=[jax.ShapeDtypeStruct((half // 2, step, n), HALF)] * 2,
        grid=(1,),
        in_specs=[first] * 4 + [flat] * 2,
        out_specs=[pl.BlockSpec((half // 2, step, n), lambda i: (0, 0, 0))] * 2,
        compiler_params=pltpu.CompilerParams(vmem_limit_bytes=14 << 20),
        cost_estimate=pl.CostEstimate(
            flops=4 * half * step * tokens * n,
            bytes_accessed=2 * half * step * (4 * tokens + n),
            transcendentals=0,
        ),
        name="weight_grads",
    )(t_sorted, t_other, g_sorted, g_other, d_own, d_other)


def part_terms_kernel(w, cotangent, out):
    step = w.shape[0] // SIDE
    for i in range(SIDE):
        at = slice(i * step, (i + 1) * step)
        out[at, :] = mm(cotangent[...], w[at, :], NT).astype(HALF)


def part_terms(weights, part, cotangent):
    rows, n = weights.shape
    rows = rows // SIDE
    tokens = cotangent.shape[0]
    return pl.pallas_call(
        part_terms_kernel,
        out_shape=jax.ShapeDtypeStruct((SIDE * tokens, rows // SIDE), HALF),
        grid=(1,),
        in_specs=[
            pl.BlockSpec((rows, n), lambda i: (part, 0)),
            pl.BlockSpec((tokens, n), lambda i: (0, 0)),
        ],
        out_specs=pl.BlockSpec((SIDE * tokens, rows // SIDE), lambda i: (0, 0)),
        compiler_params=pltpu.CompilerParams(vmem_limit_bytes=4 << 20),
        cost_estimate=pl.CostEstimate(
            flops=2 * rows * n * tokens, bytes_accessed=2 * rows * (n + tokens), transcendentals=0
        ),
        name="part_terms",
    )(weights, cotangent)


def split_sum_kernel(mine, got, q, k, v, o):
    n = q.shape[1]
    for i, out in enumerate((q, k, v, o)):
        at = slice(i * n, (i + 1) * n)
        acc = mine[:, at].astype(WIDE) + got[:, at].astype(WIDE)
        out[...] = acc if out is not o else acc.T


def split_sum(mine, got):
    rows, width = got.shape
    n = width // SIDE
    flat = pl.BlockSpec((rows, n), lambda i: (0, 0))
    tall = jax.ShapeDtypeStruct((rows, n), WIDE)
    return pl.pallas_call(
        split_sum_kernel,
        out_shape=(tall, tall, tall, jax.ShapeDtypeStruct((n, rows), WIDE)),
        grid=(1,),
        in_specs=[pl.BlockSpec((rows, width), lambda i: (0, 0))] * 2,
        out_specs=(flat, flat, flat, pl.BlockSpec((n, rows), lambda i: (0, 0))),
        compiler_params=pltpu.CompilerParams(vmem_limit_bytes=5 << 20),
        cost_estimate=pl.CostEstimate(
            flops=rows * width, bytes_accessed=8 * rows * width, transcendentals=0
        ),
        name="split_sum",
    )(mine, got)


def spread_phase1(a):
    return [a] + [plane_shift(a, 0, d) for d in range(1, SIDE)]


def spread_phase2(a):
    return [a] + [plane_shift(a, 1, d) for d in range(1, SIDE)]


def total(parts):
    acc = parts[0].astype(WIDE)
    for p in parts[1:]:
        acc = acc + p.astype(WIDE)
    return acc


def fold_phase1(terms):
    return [terms[0]] + [plane_shift(t, 1, -d) for d, t in enumerate(terms) if d]


def fold_phase2(mine):
    step = mine[0].shape[0] // SIDE
    parts = [jnp.stack([m[d * step : (d + 1) * step] for m in mine]) for d in range(SIDE)]
    return [parts[0]] + [plane_shift(p, 0, -d) for d, p in enumerate(parts) if d]


def pair_sums(own, other):
    core = lax.axis_index("core")
    pair = (own.astype(WIDE) + other.astype(WIDE)).astype(HALF)
    near, far = lax.optimization_barrier((x_outward(pair), x_shift(pair, 2)))
    across = core_swap(near)
    return [
        pair,
        jnp.where(core == 0, near, across),
        far,
        jnp.where(core == 0, across, near),
    ]


def masked_sum(first, parts, keep):
    acc = first
    for part, k in zip(parts, keep):
        acc = acc + jnp.where(k, part.astype(WIDE), 0.0)
    return acc


def rounded_sum(a, b):
    return (a.astype(WIDE) + b.astype(WIDE)).astype(HALF)


def seq_exchange(own, earlier):
    x, core = lax.axis_index("x"), lax.axis_index("core")
    other = core_swap(own)
    pair = rounded_sum(own, other)
    near = x_partner(pair, (1, 1))
    four = rounded_sum(pair, near)
    far = x_partner(four, (2, 2))
    ahead = [core == 1, x % 2 == 1, x >= 2]
    acc = jnp.zeros(own.shape, WIDE)
    for part, before in zip((other, near, far), ahead):
        keep = before if earlier else jnp.logical_not(before)
        acc = acc + jnp.where(keep, part.astype(WIDE), 0.0)
    return acc, (four, far), other


def on_device(tokens, w_query, w_key, w_value, w_out, grad_out, state_in):
    x, core = lax.axis_index("x"), lax.axis_index("core")
    dh = w_query.shape[1]
    rows = tokens.shape[0]
    table, slots = block_tables()

    t1 = jnp.concatenate(spread_phase1(tokens.T), axis=0)
    g1 = jnp.concatenate(spread_phase1(grad_out.T), axis=0)
    t1, raw = lax.optimization_barrier((t1, (w_query, w_key, w_value, w_out)))
    t_parts = spread_phase2(t1)
    w_qkv, w_o = order_weights(table, *raw)
    g_parts = spread_phase2(g1)
    step = g1.shape[0]
    wq_parts = [w_qkv[d * step : (d + 1) * step] for d in range(SIDE)]
    wo_parts = [w_o[d * step : (d + 1) * step] for d in range(SIDE)]

    qkv = sum(mm(t, w, TN) for t, w in zip(t_parts, wq_parts)).astype(HALF)
    query, keys, values = (qkv[:, i * dh : (i + 1) * dh] for i in range(3))

    own_state = mm(keys, values, TN).astype(HALF)
    other = core_swap(own_state)
    g_parts = after(other, g_parts)
    pairs = pair_sums(own_state, other)
    prior = masked_sum(
        state_in[0], [other] + pairs[1:], [core == 1] + [x >= d for d in range(1, SIDE)]
    ).astype(HALF)

    allowed = jnp.tril(jnp.ones((rows, rows), jnp.bool_))
    scores = jnp.where(allowed, mm(query, keys, NT), 0.0).astype(HALF)
    mixed = mm(scores, values, NN) + mm(query, prior, NN)
    inv_norm = lax.rsqrt(jnp.mean(mixed * mixed, axis=-1, keepdims=True) + EPSILON)
    normed = (mixed * inv_norm).astype(HALF)
    out_terms = [part_terms(w_o, d, normed) for d in range(SIDE)]
    out_got = fold_phase1(out_terms)

    grad_normed = sum(mm(g, w, TN) for g, w in zip(g_parts, wo_parts))
    grad_mixed = inv_norm * (
        grad_normed
        - mixed * inv_norm * inv_norm * jnp.mean(grad_normed * mixed, axis=-1, keepdims=True)
    )
    grad_mixed = grad_mixed.astype(HALF)
    own_back = mm(query, grad_mixed, TN).astype(HALF)
    half = SIDE * SIDE // 2
    t_sorted, g_sorted = sort_blocks(slots, t_parts), sort_blocks(slots, g_parts)
    own_back = after(out_terms, own_back)
    behind, halves, _ = seq_exchange(own_back, False)
    t_other, g_other = (core_swap(after(halves[0], a[half:])) for a in (t_sorted, g_sorted))

    grad_scores = jnp.where(allowed, mm(grad_mixed, values, NT), 0.0).astype(HALF)
    grad_query = (mm(grad_scores, keys, NN) + mm(grad_mixed, prior, NT)).astype(HALF)
    later = behind.astype(HALF)
    grad_state = total(halves)
    grad_keys = (mm(grad_scores, query, TN) + mm(values, later, NT)).astype(HALF)
    grad_values = (mm(scores, grad_mixed, TN) + mm(keys, later, NN)).astype(HALF)
    out_sum = total(out_got).astype(HALF)
    cotangents = jnp.concatenate([grad_query, grad_keys, grad_values, normed], axis=1)
    other_cotangents = core_swap(cotangents)
    cotangents, out_sum = lax.optimization_barrier((cotangents, out_sum))
    keep, send = weight_grads(
        t_sorted, t_other, g_sorted, g_other, cotangents, other_cotangents
    )
    sent = x_partner(send, (1, 3))
    in_terms = [part_terms(w_qkv, d, cotangents) for d in range(SIDE)]
    in_got = fold_phase1(in_terms)
    mine = (keep.astype(WIDE) + sent.astype(WIDE)).astype(HALF)
    mine = mine.reshape(2, -1, mine.shape[2])
    own, send = mine[0], mine[1]
    in_got = after((own, send), in_got)
    got = fold_phase2((out_sum, total(in_got).astype(HALF)))
    result = total([g[0] for g in got]).astype(HALF)
    grad_tokens = total([g[1] for g in got])
    grads = split_sum(after((result, grad_tokens), own), x_partner(send, (2, 2)))
    return (
        result,
        grad_tokens,
        *grads,
        grad_state[None],
    )


def solution(mesh):
    sizes = (SIDE, mesh.shape["seq"] // SIDE, SIDE, SIDE)
    torus = Mesh(mesh.devices.reshape(sizes), SEQ + HEAD)
    seq_head = P(SEQ, HEAD)
    column = P(None, HEAD)
    return jax.shard_map(
        on_device,
        mesh=torus,
        in_specs=(seq_head, column, column, column, P(HEAD, None), seq_head, P(HEAD, None, None)),
        out_specs=(
            seq_head,
            seq_head,
            seq_head,
            seq_head,
            seq_head,
            P(HEAD, SEQ),
            P(HEAD, None, None),
        ),
        check_vma=False,
    )
```

```python
import jax
import jax.numpy as jnp
from jax import lax
from jax.experimental import pallas as pl
from jax.experimental.pallas import tpu as pltpu
from jax.sharding import Mesh
from jax.sharding import PartitionSpec as P

SEQ = ("x", "core")
HEAD = ("y", "z")
PLANE = ("core", "y", "z")
SIDE = 4
EPSILON = 1e-06
WIDE = jnp.float32
HALF = jnp.bfloat16

NN = (((1,), (0,)), ((), ()))
NT = (((1,), (1,)), ((), ()))
TN = (((0,), (0,)), ((), ()))


def mm(a, b, dims):
    return lax.dot_general(a, b, dims, preferred_element_type=WIDE)


def after(first, then):
    return lax.optimization_barrier((first, then))[1]


def plane_pairs(phase, shift):
    pairs = []
    for core in range(2):
        for y in range(SIDE):
            for z in range(SIDE):
                along_y = core == phase
                ty = (y + shift) % SIDE if along_y else y
                tz = z if along_y else (z + shift) % SIDE
                pairs.append(((core * SIDE + y) * SIDE + z, (core * SIDE + ty) * SIDE + tz))
    return pairs


def plane_shift(a, phase, shift):
    return lax.ppermute(a, PLANE, plane_pairs(phase, shift))


def x_shift(a, shift):
    return lax.ppermute(a, "x", [(i, (i + shift) % SIDE) for i in range(SIDE)])


def x_outward(a):
    pairs = []
    for i in range(SIDE):
        pairs.append((2 * i, 2 * ((i + 1) % SIDE)))
        pairs.append((2 * i + 1, 2 * ((i - 1) % SIDE) + 1))
    return lax.ppermute(a, SEQ, pairs)


def x_partner(a, bits):
    pairs = [(2 * i + c, 2 * (i ^ bits[c]) + c) for i in range(SIDE) for c in range(2)]
    return lax.ppermute(a, SEQ, pairs)


def core_swap(a):
    return lax.ppermute(a, "core", [(0, 1), (1, 0)])


def block_tables():
    x, core, y, z = (lax.axis_index(n) for n in ("x",) + PLANE)
    at = jnp.arange(SIDE * SIDE, dtype=jnp.int32)
    d2, d1 = at // SIDE, at % SIDE
    from_y = (y - jnp.where(core == 0, d1, d2)) % SIDE
    from_z = (z - jnp.where(core == 0, d2, d1)) % SIDE
    other_core = (from_z // 2 + core) % 2
    away = x ^ from_y
    place = jnp.where(away % 2 == 0, away // 2, 2 + ((away // 2) ^ (from_z // 2)))
    slots = other_core * 8 + place * 2 + from_z % 2
    return from_y * SIDE + from_z, slots


def order_weights_kernel(table, q, k, v, o, qkv_out, o_out):
    n = q.shape[1]
    step = q.shape[0] // (SIDE * SIDE)
    for i in range(SIDE * SIDE):
        at = pl.ds(pl.multiple_of(table[i] * step, step), step)
        to = slice(i * step, (i + 1) * step)
        qkv_out[to, :n] = q[at, :]
        qkv_out[to, n : 2 * n] = k[at, :]
        qkv_out[to, 2 * n :] = v[at, :]
        o_out[to, :] = o[:, at].T


def order_weights(table, w_query, w_key, w_value, w_out):
    rows, n = w_query.shape
    tall = pl.BlockSpec((rows, n), lambda i: (0, 0))
    return pl.pallas_call(
        order_weights_kernel,
        out_shape=(
            jax.ShapeDtypeStruct((rows, 3 * n), HALF),
            jax.ShapeDtypeStruct((rows, n), HALF),
        ),
        grid=(1,),
        in_specs=[pl.BlockSpec(memory_space=pltpu.SMEM), tall, tall, tall]
        + [pl.BlockSpec((n, rows), lambda i: (0, 0))],
        out_specs=(pl.BlockSpec((rows, 3 * n), lambda i: (0, 0)), tall),
        compiler_params=pltpu.CompilerParams(vmem_limit_bytes=18 << 20),
        cost_estimate=pl.CostEstimate(
            flops=0, bytes_accessed=16 * rows * n, transcendentals=0
        ),
        name="order_weights",
    )(table, w_query, w_key, w_value, w_out)


def sort_blocks_kernel(slots, a0, a1, a2, a3, out):
    step = a0.shape[0] // SIDE
    for d2, part in enumerate((a0, a1, a2, a3)):
        for d1 in range(SIDE):
            out[slots[d2 * SIDE + d1]] = part[d1 * step : (d1 + 1) * step, :]


def sort_blocks(slots, parts):
    rows, n = parts[0].shape
    shape = (SIDE * SIDE, rows // SIDE, n)
    return pl.pallas_call(
        sort_blocks_kernel,
        out_shape=jax.ShapeDtypeStruct(shape, HALF),
        grid=(1,),
        in_specs=[pl.BlockSpec(memory_space=pltpu.SMEM)]
        + [pl.BlockSpec((rows, n), lambda i: (0, 0))] * SIDE,
        out_specs=pl.BlockSpec(shape, lambda i: (0, 0, 0)),
        compiler_params=pltpu.CompilerParams(vmem_limit_bytes=9 << 20),
        cost_estimate=pl.CostEstimate(
            flops=0, bytes_accessed=16 * rows * n, transcendentals=0
        ),
        name="sort_blocks",
    )(slots, *parts)


def weight_grads_kernel(t_own, t_other, g_own, g_other, d_own, d_other, keep, send):
    n = d_own.shape[1]
    half = keep.shape[0]
    split = n - n // SIDE
    for s in range(t_own.shape[0]):
        for own, other, at in ((t_own, t_other, slice(0, split)), (g_own, g_other, slice(split, n))):
            term = jnp.dot(own[s], d_own[:, at], preferred_element_type=WIDE)
            term = term + jnp.dot(other[s], d_other[:, at], preferred_element_type=WIDE)
            if s < half:
                keep[s, :, at] = term.astype(HALF)
            else:
                send[s - half, :, at] = term.astype(HALF)


def weight_grads(t_sorted, t_other, g_sorted, g_other, d_own, d_other):
    half, step, tokens = t_other.shape
    n = d_own.shape[1]
    first = pl.BlockSpec((half, step, tokens), lambda i: (0, 0, 0))
    flat = pl.BlockSpec((tokens, n), lambda i: (0, 0))
    return pl.pallas_call(
        weight_grads_kernel,
        out_shape=[jax.ShapeDtypeStruct((half // 2, step, n), HALF)] * 2,
        grid=(1,),
        in_specs=[first] * 4 + [flat] * 2,
        out_specs=[pl.BlockSpec((half // 2, step, n), lambda i: (0, 0, 0))] * 2,
        compiler_params=pltpu.CompilerParams(vmem_limit_bytes=14 << 20),
        cost_estimate=pl.CostEstimate(
            flops=4 * half * step * tokens * n,
            bytes_accessed=2 * half * step * (4 * tokens + n),
            transcendentals=0,
        ),
        name="weight_grads",
    )(t_sorted, t_other, g_sorted, g_other, d_own, d_other)


def part_terms_kernel(w, cotangent, out):
    step = w.shape[0] // SIDE
    for i in range(SIDE):
        at = slice(i * step, (i + 1) * step)
        out[at, :] = mm(cotangent[...], w[at, :], NT).astype(HALF)


def part_terms(weights, part, cotangent):
    rows, n = weights.shape
    rows = rows // SIDE
    tokens = cotangent.shape[0]
    return pl.pallas_call(
        part_terms_kernel,
        out_shape=jax.ShapeDtypeStruct((SIDE * tokens, rows // SIDE), HALF),
        grid=(1,),
        in_specs=[
            pl.BlockSpec((rows, n), lambda i: (part, 0)),
            pl.BlockSpec((tokens, n), lambda i: (0, 0)),
        ],
        out_specs=pl.BlockSpec((SIDE * tokens, rows // SIDE), lambda i: (0, 0)),
        compiler_params=pltpu.CompilerParams(vmem_limit_bytes=4 << 20),
        cost_estimate=pl.CostEstimate(
            flops=2 * rows * n * tokens, bytes_accessed=2 * rows * (n + tokens), transcendentals=0
        ),
        name="part_terms",
    )(weights, cotangent)


def split_sum_kernel(mine, got, q, k, v, o):
    n = q.shape[1]
    for i, out in enumerate((q, k, v, o)):
        at = slice(i * n, (i + 1) * n)
        acc = mine[:, at].astype(WIDE) + got[:, at].astype(WIDE)
        out[...] = acc if out is not o else acc.T


def split_sum(mine, got):
    rows, width = got.shape
    n = width // SIDE
    flat = pl.BlockSpec((rows, n), lambda i: (0, 0))
    tall = jax.ShapeDtypeStruct((rows, n), WIDE)
    return pl.pallas_call(
        split_sum_kernel,
        out_shape=(tall, tall, tall, jax.ShapeDtypeStruct((n, rows), WIDE)),
        grid=(1,),
        in_specs=[pl.BlockSpec((rows, width), lambda i: (0, 0))] * 2,
        out_specs=(flat, flat, flat, pl.BlockSpec((n, rows), lambda i: (0, 0))),
        compiler_params=pltpu.CompilerParams(vmem_limit_bytes=5 << 20),
        cost_estimate=pl.CostEstimate(
            flops=rows * width, bytes_accessed=8 * rows * width, transcendentals=0
        ),
        name="split_sum",
    )(mine, got)


def spread_phase1(a):
    return [a] + [plane_shift(a, 0, d) for d in range(1, SIDE)]


def spread_phase2(a):
    return [a] + [plane_shift(a, 1, d) for d in range(1, SIDE)]


def total(parts):
    acc = parts[0].astype(WIDE)
    for p in parts[1:]:
        acc = acc + p.astype(WIDE)
    return acc


def fold_phase1(terms):
    return [terms[0]] + [plane_shift(t, 1, -d) for d, t in enumerate(terms) if d]


def fold_phase2(mine):
    step = mine[0].shape[0] // SIDE
    parts = [jnp.stack([m[d * step : (d + 1) * step] for m in mine]) for d in range(SIDE)]
    return [parts[0]] + [plane_shift(p, 0, -d) for d, p in enumerate(parts) if d]


def pair_sums(own, other):
    core = lax.axis_index("core")
    pair = (own.astype(WIDE) + other.astype(WIDE)).astype(HALF)
    near, far = lax.optimization_barrier((x_outward(pair), x_shift(pair, 2)))
    across = core_swap(near)
    return [
        pair,
        jnp.where(core == 0, near, across),
        far,
        jnp.where(core == 0, across, near),
    ]


def masked_sum(first, parts, keep):
    acc = first
    for part, k in zip(parts, keep):
        acc = acc + jnp.where(k, part.astype(WIDE), 0.0)
    return acc


def rounded_sum(a, b):
    return (a.astype(WIDE) + b.astype(WIDE)).astype(HALF)


def seq_exchange(own, earlier, first):
    x, core = lax.axis_index("x"), lax.axis_index("core")
    other = core_swap(own)
    pair = after(first, rounded_sum(own, other))
    near = x_partner(pair, (1, 1))
    four = rounded_sum(pair, near)
    far = x_partner(four, (2, 2))
    ahead = [core == 1, x % 2 == 1, x >= 2]
    acc = jnp.zeros(own.shape, WIDE)
    for part, before in zip((other, near, far), ahead):
        keep = before if earlier else jnp.logical_not(before)
        acc = acc + jnp.where(keep, part.astype(WIDE), 0.0)
    return acc, (four, far), other


def on_device(tokens, w_query, w_key, w_value, w_out, grad_out, state_in):
    x, core = lax.axis_index("x"), lax.axis_index("core")
    dh = w_query.shape[1]
    rows = tokens.shape[0]
    table, slots = block_tables()

    t1 = jnp.concatenate(spread_phase1(tokens.T), axis=0)
    g1 = jnp.concatenate(spread_phase1(grad_out.T), axis=0)
    t1, raw = lax.optimization_barrier((t1, (w_query, w_key, w_value, w_out)))
    t_parts = spread_phase2(t1)
    w_qkv, w_o = order_weights(table, *raw)
    g_parts = spread_phase2(g1)
    step = g1.shape[0]
    wq_parts = [w_qkv[d * step : (d + 1) * step] for d in range(SIDE)]
    wo_parts = [w_o[d * step : (d + 1) * step] for d in range(SIDE)]

    qkv = sum(mm(t, w, TN) for t, w in zip(t_parts, wq_parts)).astype(HALF)
    query, keys, values = (qkv[:, i * dh : (i + 1) * dh] for i in range(3))

    own_state = mm(keys, values, TN).astype(HALF)
    other = core_swap(own_state)
    g_parts = after(other, g_parts)
    pairs = pair_sums(own_state, other)
    prior = masked_sum(
        state_in[0], [other] + pairs[1:], [core == 1] + [x >= d for d in range(1, SIDE)]
    ).astype(HALF)

    allowed = jnp.tril(jnp.ones((rows, rows), jnp.bool_))
    scores = jnp.where(allowed, mm(query, keys, NT), 0.0).astype(HALF)
    mixed = mm(scores, values, NN) + mm(query, prior, NN)
    inv_norm = lax.rsqrt(jnp.mean(mixed * mixed, axis=-1, keepdims=True) + EPSILON)
    normed = (mixed * inv_norm).astype(HALF)

    grad_normed = sum(mm(g, w, TN) for g, w in zip(g_parts, wo_parts))
    grad_mixed = inv_norm * (
        grad_normed
        - mixed * inv_norm * inv_norm * jnp.mean(grad_normed * mixed, axis=-1, keepdims=True)
    )
    grad_mixed = grad_mixed.astype(HALF)
    own_back = mm(query, grad_mixed, TN).astype(HALF)
    out_terms = [part_terms(w_o, d, after(own_back, normed)) for d in range(SIDE)]
    out_got = fold_phase1(out_terms)
    half = SIDE * SIDE // 2
    t_sorted, g_sorted = sort_blocks(slots, t_parts), sort_blocks(slots, g_parts)
    behind, halves, _ = seq_exchange(own_back, False, out_terms)
    t_other, g_other = (core_swap(after(halves[0], a[half:])) for a in (t_sorted, g_sorted))

    grad_scores = jnp.where(allowed, mm(grad_mixed, values, NT), 0.0).astype(HALF)
    grad_query = (mm(grad_scores, keys, NN) + mm(grad_mixed, prior, NT)).astype(HALF)
    later = behind.astype(HALF)
    grad_state = total(halves)
    grad_keys = (mm(grad_scores, query, TN) + mm(values, later, NT)).astype(HALF)
    grad_values = (mm(scores, grad_mixed, TN) + mm(keys, later, NN)).astype(HALF)
    out_sum = total(out_got).astype(HALF)
    cotangents = jnp.concatenate([grad_query, grad_keys, grad_values, normed], axis=1)
    other_cotangents = core_swap(cotangents)
    cotangents, out_sum = lax.optimization_barrier((cotangents, out_sum))
    keep, send = weight_grads(
        t_sorted, t_other, g_sorted, g_other, cotangents, other_cotangents
    )
    sent = x_partner(send, (1, 3))
    in_terms = [part_terms(w_qkv, d, cotangents) for d in range(SIDE)]
    in_got = fold_phase1(in_terms)
    mine = (keep.astype(WIDE) + sent.astype(WIDE)).astype(HALF)
    mine = mine.reshape(2, -1, mine.shape[2])
    own, send = mine[0], mine[1]
    in_got = after((own, send), in_got)
    got = fold_phase2((out_sum, total(in_got).astype(HALF)))
    grads = split_sum(after(got[1], own), x_partner(send, (2, 2)))
    got[3] = after(grads, got[3])
    result = total([g[0] for g in got]).astype(HALF)
    grad_tokens = total([g[1] for g in got])
    return (
        result,
        grad_tokens,
        *grads,
        grad_state[None],
    )


def solution(mesh):
    sizes = (SIDE, mesh.shape["seq"] // SIDE, SIDE, SIDE)
    torus = Mesh(mesh.devices.reshape(sizes), SEQ + HEAD)
    seq_head = P(SEQ, HEAD)
    column = P(None, HEAD)
    return jax.shard_map(
        on_device,
        mesh=torus,
        in_specs=(seq_head, column, column, column, P(HEAD, None), seq_head, P(HEAD, None, None)),
        out_specs=(
            seq_head,
            seq_head,
            seq_head,
            seq_head,
            seq_head,
            P(HEAD, SEQ),
            P(HEAD, None, None),
        ),
        check_vma=False,
    )
```
